32 devices in a mesh: groups: 2 (over y), weight: 4 (over z), token: 2 (over x), sub: 2 (over core).
Axes of the slice: x: 2, y: 2, z: 4, core: 2. Of those that a mesh axis runs over, the one named last changes fastest.
Arguments:
- tokens: bfloat16 [512, 8192], P(('groups', 'token'), ('weight', 'sub')), parts along dimension 0, may hold values from -6 to 6
- gate_blocks: bfloat16 [2, 8, 384, 128, 128], P('token', ('weight', 'sub')), may hold values from -0.09375 to 0.09375
- up_blocks: bfloat16 [2, 8, 384, 128, 128], P('token', ('weight', 'sub')), may hold values from -0.09375 to 0.09375
- gate_list: int32 [2, 8, 384], P(None, ('weight', 'sub')), may hold values from 0 to 511, as said below
- gate_count: int32 [2, 8], P(None, ('weight', 'sub')), may hold values from 128 to 384, as said below
- up_list: int32 [2, 8, 384], P(None, ('weight', 'sub')), may hold values from 0 to 511, as said below
- up_count: int32 [2, 8], P(None, ('weight', 'sub')), may hold values from 128 to 384, as said below
- cotangent: bfloat16 [512, 16384], P(('groups', 'token'), ('weight', 'sub')), parts along dimension 0, may hold values from -0.375 to 0.375
Outputs:
- hidden: bfloat16 [512, 16384], P(('groups', 'token'), ('weight', 'sub')), parts along dimension 0
- gate_grad: bfloat16 [4, 8, 384, 128, 128], P(('groups', 'token'), ('weight', 'sub')), parts along dimension 0
- up_grad: bfloat16 [4, 8, 384, 128, 128], P(('groups', 'token'), ('weight', 'sub')), parts along dimension 0
The draws below stay inside these ranges and needn't reach their ends.
There are 2 independent parts, one for each index of `groups`. The reference program is written for one: setup_inputs(seed, part) draws one part's arguments, and reference() takes and returns one part's arrays. A program takes and returns all parts, laid end to end along the dimension named above; an argument that names none is the same for every part. Nothing has to cross between parts.
Inputs may be any that keep to these rules, and one draw needn't show every extreme that they name: `gate_list`: the 384 entries of one owner are distinct block positions. `up_list`: the 384 entries of one owner are distinct block positions. The first gate_count[t, c] slots of owner (t, c) are live; some owner has exactly 384. The first up_count[t, c] slots of owner (t, c) are live; some owner has exactly 384.
All inputs are finite; a program needn't handle non-finite values.
Results may differ from the reference program's by a relative error of at most 0.0059.
Values may be sent and summed in bfloat16 or wider, within the bound.
A program may use at most 448 MiB of HBM per device.

```python
import jax
import jax.numpy as jnp
from jax import lax

D = 8192
FF = 16384
BLK = 128
TOKENS = 256
PANELS = 8
BPOS = 512
CAP = 384
N_TOKEN = 2


def list_draw(base_key):
    owner_keys = jax.random.split(base_key, N_TOKEN * PANELS)

    def one_owner(owner_key):
        return jax.random.permutation(owner_key, BPOS)[:CAP]
    permuted = jax.vmap(one_owner)(owner_keys)
    return permuted.astype(jnp.int32).reshape(N_TOKEN, PANELS, CAP)


def count_draw(base_key):
    counted = jax.random.randint(base_key, (N_TOKEN * PANELS,), BPOS - CAP, CAP + 1, dtype=jnp.int32)
    chosen = jax.random.randint(jax.random.fold_in(base_key, 7), (), 0, N_TOKEN * PANELS, dtype=jnp.int32)
    flattened = jnp.where(jnp.arange(N_TOKEN * PANELS, dtype=jnp.int32) == chosen, CAP, counted)
    return flattened.astype(jnp.int32).reshape(N_TOKEN, PANELS)


def draw_gate_list(key, part):
    return list_draw(jax.random.fold_in(key, 11))


def draw_up_list(key, part):
    return list_draw(jax.random.fold_in(key, 12))


def draw_gate_count(key, part):
    return count_draw(jax.random.fold_in(key, 21))


def draw_up_count(key, part):
    return count_draw(jax.random.fold_in(key, 22))


def level_of(key, dims, cuts, least, high):
    gain, own = 1.0, jax.random.fold_in(key, 6)
    for position, parts in cuts:
        draws = jnp.exp(jax.random.uniform(jax.random.fold_in(own, position), (parts,), jnp.float32, least / len(cuts), high / len(cuts)))
        gain = gain * jnp.repeat(draws, dims[position] // parts).reshape([-1 if axis == position else 1 for axis in range(len(dims))])
    return gain


def bell_draw(stream_key, extent, spread, bound, cuts=(), held_as=jnp.bfloat16):
    result = jax.random.normal(stream_key, extent, jnp.float32) * spread
    if len(cuts) > 0:
        result = level_of(stream_key, extent, cuts, -0.22, 0.18) * result
    return jnp.clip(result, min=-bound, max=bound).astype(held_as)


def setup_inputs(seed: int = 0, part: int = 0) -> dict:
    arg_keys = jax.random.split(jax.random.key(seed), 9)
    part_keys = jax.random.split(jax.random.fold_in(arg_keys[8], part), 9)
    tokens = bell_draw(part_keys[0], (TOKENS, D), 1.0, 6.0, ((0, 2), (1, 8)))
    gate_blocks = bell_draw(arg_keys[1], (N_TOKEN, PANELS, CAP, BLK, BLK), (D // 2) ** -0.5, 0.09375, ((0, 2), (1, 8)))
    up_blocks = bell_draw(arg_keys[2], (N_TOKEN, PANELS, CAP, BLK, BLK), (D // 2) ** -0.5, 0.09375, ((0, 2), (1, 8)))
    gate_list = draw_gate_list(jax.random.fold_in(arg_keys[8], 71), part)
    gate_count = draw_gate_count(jax.random.fold_in(arg_keys[8], 71), part)
    up_list = draw_up_list(jax.random.fold_in(arg_keys[8], 71), part)
    up_count = draw_up_count(jax.random.fold_in(arg_keys[8], 71), part)
    cotangent = bell_draw(part_keys[7], (TOKENS, FF), (TOKENS ** -0.5), 0.375, ((0, 2), (1, 8)))
    return {"tokens": tokens, "gate_blocks": gate_blocks, "up_blocks": up_blocks, "gate_list": gate_list, "gate_count": gate_count, "up_list": up_list, "up_count": up_count, "cotangent": cotangent}


def expand(blocks, slot_lists, slot_counts):
    n_owner_rows, n_panels, capacity = slot_lists.shape
    row_blocks = D // BLK // n_owner_rows
    col_blocks = FF // BLK // n_panels
    live_slots = jnp.arange(capacity, dtype=jnp.int32)[None, None, :] < slot_counts[:, :, None]
    kept_blocks = jnp.where(live_slots[..., None, None], blocks, jnp.zeros_like(blocks))
    dense_matrix = jnp.zeros((n_owner_rows, n_panels, row_blocks * col_blocks, BLK, BLK), blocks.dtype)
    owner_rows = jnp.arange(n_owner_rows, dtype=jnp.int32)[:, None, None]
    owner_cols = jnp.arange(n_panels, dtype=jnp.int32)[None, :, None]
    dense_matrix = dense_matrix.at[owner_rows, owner_cols, slot_lists].set(kept_blocks)
    dense_matrix = dense_matrix.reshape(n_owner_rows, n_panels, row_blocks, col_blocks, BLK, BLK)
    return dense_matrix.transpose(0, 2, 4, 1, 3, 5).reshape(D, FF)

def block_grad(tokens, delta, slot_lists, slot_counts):
    n_owner_rows, n_panels, capacity = slot_lists.shape
    row_blocks = D // BLK // n_owner_rows
    col_blocks = FF // BLK // n_panels
    group_rows = tokens.reshape(n_owner_rows, -1, D)
    group_deltas = delta.reshape(n_owner_rows, -1, FF)

    def add_group(running, group_pair):
        group_term = jnp.dot(group_pair[0].T, group_pair[1], preferred_element_type=jnp.float32)
        group_term = lax.optimization_barrier(group_term.astype(jnp.bfloat16))
        return (running + group_term.astype(jnp.float32), None)
    running, _ = lax.scan(add_group, jnp.zeros((D, FF), jnp.float32), (group_rows, group_deltas))
    arranged = running.reshape(n_owner_rows, row_blocks, BLK, n_panels, col_blocks, BLK)
    arranged = arranged.transpose(0, 3, 1, 4, 2, 5).reshape(n_owner_rows, n_panels, row_blocks * col_blocks, BLK, BLK)
    selected = jnp.take_along_axis(arranged, slot_lists[:, :, :, None, None], axis=2)
    live_slots = jnp.arange(capacity, dtype=jnp.int32)[None, None, :] < slot_counts[:, :, None]
    return jnp.where(live_slots[..., None, None], selected, jnp.zeros_like(selected)).astype(jnp.bfloat16)

def reference(tokens, gate_blocks, up_blocks, gate_list, gate_count, up_list, up_count, cotangent):
    gate_weight = expand(gate_blocks, gate_list, gate_count)
    up_weight = expand(up_blocks, up_list, up_count)
    gate_sum = jnp.dot(tokens, gate_weight, preferred_element_type=jnp.float32)
    up_sum = jnp.dot(tokens, up_weight, preferred_element_type=jnp.float32)
    sigmoid_gate = jax.nn.sigmoid(gate_sum)
    silu_gate = gate_sum * sigmoid_gate
    hidden = (silu_gate * up_sum).astype(jnp.bfloat16)
    cot_values = cotangent.astype(jnp.float32)
    gate_delta = (cot_values * up_sum * sigmoid_gate * (1.0 + gate_sum * (1.0 - sigmoid_gate))).astype(jnp.bfloat16)
    up_delta = (cot_values * silu_gate).astype(jnp.bfloat16)
    gate_grad = block_grad(tokens, gate_delta, gate_list, gate_count)
    up_grad = block_grad(tokens, up_delta, up_list, up_count)
    return (hidden, gate_grad, up_grad)
```

```python
import functools

import jax
import jax.numpy as jnp
from jax import lax
from jax.experimental import pallas as pl
from jax.experimental.pallas import tpu as pltpu
from jax.sharding import PartitionSpec as P


def place_kernel(
    lists, counts, gate_blocks, up_blocks, placed, dense, blank, block_sems, out_sems
):
    capacity, block, _ = gate_blocks.shape
    depth, both = dense.shape
    width = both // 2
    cols = width // block
    strip = min(depth, 256)
    blank[...] = jnp.zeros_like(blank)
    sources = (gate_blocks, up_blocks)
    for m, source in enumerate(sources):

        @pl.loop(0, depth // strip)
        def _(i):
            rows = pl.ds(pl.multiple_of(i * strip, strip), strip)
            dense[rows, m * width : (m + 1) * width] = jnp.zeros((strip, width), dense.dtype)

        @pl.loop(0, capacity)
        def _(k):
            position = lists[m, k]
            row = pl.multiple_of(lax.div(position, cols) * block, block)
            col = pl.multiple_of(m * width + lax.rem(position, cols) * block, block)
            target = dense.at[pl.ds(row, block), pl.ds(col, block)]
            live = k < counts[m]

            @pl.when(live)
            def _():
                pltpu.make_async_copy(source.at[k], target, block_sems.at[m]).start()

            @pl.when(jnp.logical_not(live))
            def _():
                pltpu.make_async_copy(blank, target, block_sems.at[m]).start()

    writes = []
    for m, source in enumerate(sources):
        pltpu.make_async_copy(source, source, block_sems.at[m]).wait()
        half = pl.ds(m * width, width)
        write = pltpu.make_async_copy(dense.at[:, half], placed.at[:, half], out_sems.at[m])
        write.start()
        writes.append(write)
    for write in writes:
        write.wait()


def place(lists, counts, gate_blocks, up_blocks, depth, width):
    block = gate_blocks.shape[1]
    return pl.pallas_call(
        place_kernel,
        out_shape=jax.ShapeDtypeStruct((depth, 2 * width), gate_blocks.dtype),
        in_specs=[
            pl.BlockSpec(memory_space=pltpu.SMEM),
            pl.BlockSpec(memory_space=pltpu.SMEM),
            pl.BlockSpec(memory_space=pl.ANY),
            pl.BlockSpec(memory_space=pl.ANY),
        ],
        out_specs=pl.BlockSpec(memory_space=pl.ANY),
        scratch_shapes=[
            pltpu.VMEM((depth, 2 * width), gate_blocks.dtype),
            pltpu.VMEM((block, block), gate_blocks.dtype),
            pltpu.SemaphoreType.DMA((2,)),
            pltpu.SemaphoreType.DMA((2,)),
        ],
        compiler_params=pltpu.CompilerParams(vmem_limit_bytes=50 << 20),
        cost_estimate=pl.CostEstimate(
            flops=0, bytes_accessed=2 * gate_blocks.size * 2 + depth * width * 4, transcendentals=0
        ),
    )(lists, counts, gate_blocks, up_blocks)


def grad_kernel(lists, counts, turned, delta, gate_grad, up_grad, dense, sems):
    capacity, block, _ = gate_grad.shape
    depth = turned.shape[0]
    width = delta.shape[1] // 2
    cols = width // block
    strip = min(depth, 256)
    piece = min(width, 512)
    outs = (gate_grad, up_grad)
    for m, out in enumerate(outs):
        dense[m, depth : depth + block, 0:block] = jnp.zeros((block, block), dense.dtype)

        @pl.loop(0, depth // strip)
        def _(i):
            rows = pl.ds(pl.multiple_of(i * strip, strip), strip)
            for j in range(0, width, piece):
                dense[m, rows, j : j + piece] = jnp.dot(
                    turned[rows, :],
                    delta[:, m * width + j : m * width + j + piece],
                    preferred_element_type=jnp.float32,
                ).astype(dense.dtype)

        @pl.loop(0, capacity)
        def _(k):
            position = lists[m, k]
            live = k < counts[m]
            row = jnp.where(live, lax.div(position, cols) * block, depth)
            col = jnp.where(live, lax.rem(position, cols) * block, 0)
            source = dense.at[
                m, pl.ds(pl.multiple_of(row, block), block), pl.ds(pl.multiple_of(col, block), block)
            ]
            pltpu.make_async_copy(source, out.at[k], sems.at[m]).start()

    for m, out in enumerate(outs):
        pltpu.make_async_copy(out, out, sems.at[m]).wait()


def block_grads(lists, counts, turned, delta, capacity, block):
    depth = turned.shape[0]
    width = delta.shape[1] // 2
    shape = jax.ShapeDtypeStruct((capacity, block, block), jnp.bfloat16)
    return pl.pallas_call(
        grad_kernel,
        out_shape=(shape, shape),
        in_specs=[
            pl.BlockSpec(memory_space=pltpu.SMEM),
            pl.BlockSpec(memory_space=pltpu.SMEM),
            pl.BlockSpec(memory_space=pltpu.VMEM),
            pl.BlockSpec(memory_space=pltpu.VMEM),
        ],
        out_specs=(pl.BlockSpec(memory_space=pl.ANY), pl.BlockSpec(memory_space=pl.ANY)),
        scratch_shapes=[
            pltpu.VMEM((2, depth + block, width), jnp.bfloat16),
            pltpu.SemaphoreType.DMA((2,)),
        ],
        compiler_params=pltpu.CompilerParams(vmem_limit_bytes=56 << 20),
        cost_estimate=pl.CostEstimate(
            flops=4 * depth * width * turned.shape[1],
            bytes_accessed=4 * capacity * block * block,
            transcendentals=0,
        ),
    )(lists, counts, turned, delta)


def shards(tokens, gate_blocks, up_blocks, gate_list, gate_count, up_list, up_count, cotangent):
    owners = lax.axis_size("token")
    me = lax.axis_index("token")
    capacity, block = gate_blocks.shape[2:4]
    rows = tokens.shape[0]
    width = cotangent.shape[1]
    model = tokens.shape[1] * lax.axis_size("weight") * lax.axis_size("sub")
    depth = model // owners
    lists = jnp.stack([gate_list[me, 0], up_list[me, 0]])
    counts = jnp.stack([gate_count[me, 0], up_count[me, 0]])

    features = lax.all_gather(tokens, ("weight", "sub"), axis=1, tiled=True)
    placed = place(lists, counts, gate_blocks[0, 0], up_blocks[0, 0], depth, width)
    slices = lax.all_to_all(features, "token", split_axis=1, concat_axis=0, tiled=True)
    turned = slices.T

    partial = jnp.dot(slices, placed, preferred_element_type=jnp.float32)
    own = lax.dynamic_slice_in_dim(partial, me * rows, rows, axis=0)
    parts = lax.all_to_all(
        partial.astype(jnp.bfloat16), "token", split_axis=0, concat_axis=0, tiled=True
    ).reshape(owners, rows, 2 * width)
    sums = own
    for s in range(owners):
        sums = sums + jnp.where(me == s, 0.0, parts[s].astype(jnp.float32))
    gate, up = sums[:, :width], sums[:, width:]
    sigmoid = jax.nn.sigmoid(gate)
    silu = gate * sigmoid
    hidden = (silu * up).astype(jnp.bfloat16)
    cot = cotangent.astype(jnp.float32)
    gate_delta = (cot * up * sigmoid * (1.0 + gate * (1.0 - sigmoid))).astype(jnp.bfloat16)
    up_delta = (cot * silu).astype(jnp.bfloat16)
    delta = jnp.concatenate([gate_delta, up_delta], axis=1)
    delta = lax.all_gather(delta, "token", axis=0, tiled=True)
    gate_grad, up_grad = block_grads(lists, counts, turned, delta, capacity, block)
    shape = (1, 1, capacity, block, block)
    return (hidden, gate_grad.reshape(shape), up_grad.reshape(shape))


def solution(mesh):
    return jax.shard_map(
        shards,
        mesh=mesh,
        in_specs=(
            P(("groups", "token"), ("weight", "sub")),
            P("token", ("weight", "sub"), None, None, None),
            P("token", ("weight", "sub"), None, None, None),
            P(None, ("weight", "sub"), None),
            P(None, ("weight", "sub")),
            P(None, ("weight", "sub"), None),
            P(None, ("weight", "sub")),
            P(("groups", "token"), ("weight", "sub")),
        ),
        out_specs=(
            P(("groups", "token"), ("weight", "sub")),
            P(("groups", "token"), ("weight", "sub"), None, None, None),
            P(("groups", "token"), ("weight", "sub"), None, None, None),
        ),
        check_vma=False,
    )
```

```python
import jax
import jax.numpy as jnp
from jax import lax
from jax.experimental import pallas as pl
from jax.experimental.pallas import tpu as pltpu
from jax.sharding import PartitionSpec as P

MESH = pl.DeviceIdType.MESH


def place_kernel(
    lists, counts, gate_blocks, up_blocks, placed, dense, blank, block_sems, out_sems
):
    capacity, block, _ = gate_blocks.shape
    depth, both = dense.shape
    width = both // 2
    cols = width // block
    strip = min(depth, 256)
    blank[...] = jnp.zeros_like(blank)
    sources = (gate_blocks, up_blocks)
    for m, source in enumerate(sources):

        @pl.loop(0, depth // strip)
        def _(i):
            rows = pl.ds(pl.multiple_of(i * strip, strip), strip)
            dense[rows, m * width : (m + 1) * width] = jnp.zeros((strip, width), dense.dtype)

        @pl.loop(0, capacity)
        def _(k):
            position = lists[m, k]
            row = pl.multiple_of(lax.div(position, cols) * block, block)
            col = pl.multiple_of(m * width + lax.rem(position, cols) * block, block)
            target = dense.at[pl.ds(row, block), pl.ds(col, block)]
            live = k < counts[m]

            @pl.when(live)
            def _():
                pltpu.make_async_copy(source.at[k], target, block_sems.at[m]).start()

            @pl.when(jnp.logical_not(live))
            def _():
                pltpu.make_async_copy(blank, target, block_sems.at[m]).start()

    writes = []
    for m, source in enumerate(sources):
        pltpu.make_async_copy(source, source, block_sems.at[m]).wait()
        half = pl.ds(m * width, width)
        write = pltpu.make_async_copy(dense.at[:, half], placed.at[:, half], out_sems.at[m])
        write.start()
        writes.append(write)
    for write in writes:
        write.wait()


def place(lists, counts, gate_blocks, up_blocks, depth, width):
    block = gate_blocks.shape[1]
    return pl.pallas_call(
        place_kernel,
        out_shape=jax.ShapeDtypeStruct((depth, 2 * width), gate_blocks.dtype),
        in_specs=[
            pl.BlockSpec(memory_space=pltpu.SMEM),
            pl.BlockSpec(memory_space=pltpu.SMEM),
            pl.BlockSpec(memory_space=pl.ANY),
            pl.BlockSpec(memory_space=pl.ANY),
        ],
        out_specs=pl.BlockSpec(memory_space=pl.ANY),
        scratch_shapes=[
            pltpu.VMEM((depth, 2 * width), gate_blocks.dtype),
            pltpu.VMEM((block, block), gate_blocks.dtype),
            pltpu.SemaphoreType.DMA((2,)),
            pltpu.SemaphoreType.DMA((2,)),
        ],
        compiler_params=pltpu.CompilerParams(vmem_limit_bytes=50 << 20),
        cost_estimate=pl.CostEstimate(
            flops=0, bytes_accessed=2 * gate_blocks.size * 2 + depth * width * 4, transcendentals=0
        ),
    )(lists, counts, gate_blocks, up_blocks)


def exchange_kernel(
    features, placed, cotangent, hidden, turned, delta,
    weights, x_all, flipped, own, sent, landed, delta_all, hidden_all,
    w_sems, x_send, x_recv, pass_send, pass_recv, p_send, p_recv, d_send, d_recv, out_sems,
):
    owners = lax.axis_size("token")
    me = lax.axis_index("token")
    sub = lax.axis_index("sub")
    rows, depth = x_all.shape[1:]
    chunks, _, pair = delta_all.shape
    piece = pair // 2
    width = chunks * piece
    half = rows // 2
    sibling = {"sub": 1 - sub}
    ahead = [{"token": lax.rem(me + d, owners)} for d in range(owners)]
    behind = [{"token": lax.rem(me + owners - d, owners)} for d in range(owners)]

    barrier = pltpu.get_barrier_semaphore()
    for d in range(1, owners):
        pl.semaphore_signal(barrier, inc=1, device_id=ahead[d], device_id_type=MESH)
    pl.semaphore_signal(barrier, inc=1, device_id=sibling, device_id_type=MESH)

    def weight_copy(c, m):
        cols = pl.ds(pl.multiple_of(m * width + c * piece, piece), piece)
        return pltpu.make_async_copy(placed.at[:, cols], weights.at[:, cols], w_sems.at[c, m])

    mine = pltpu.make_async_copy(
        features.at[:, pl.ds(pl.multiple_of(me * depth, depth), depth)], x_all.at[0], out_sems.at[0]
    )
    mine.start()
    for m in range(2):
        weight_copy(0, m).start()
    pl.semaphore_wait(barrier, owners)

    share = pl.ds(pl.multiple_of(sub * half, half), half)
    x_copies = []
    for d in range(1, owners):
        start = pl.multiple_of(lax.rem(me + d, owners) * depth, depth)
        copy = pltpu.make_async_remote_copy(
            src_ref=features.at[share, pl.ds(start, depth)],
            dst_ref=x_all.at[d, share, :],
            send_sem=x_send.at[d],
            recv_sem=x_recv.at[d],
            device_id=ahead[d],
            device_id_type=MESH,
        )
        copy.start()
        x_copies.append(copy)

    @pl.loop(1, chunks)
    def _(c):
        for m in range(2):
            weight_copy(c, m).start()

    mine.wait()

    def product(slot, c, m):
        cols = pl.ds(pl.multiple_of(m * width + c * piece, piece), piece)
        return jnp.dot(x_all[slot], weights[:, cols], preferred_element_type=jnp.float32)

    @pl.loop(0, chunks)
    def _(c):
        for m in range(2):
            weight_copy(c, m).wait()
            own[c, :, m * piece : (m + 1) * piece] = product(0, c, m)

    passes = []
    for d in range(1, owners):
        x_copies[d - 1].wait_recv()
        copy = pltpu.make_async_remote_copy(
            src_ref=x_all.at[d, share, :],
            dst_ref=x_all.at[d, share, :],
            send_sem=pass_send.at[d],
            recv_sem=pass_recv.at[d],
            device_id=sibling,
            device_id_type=MESH,
        )
        copy.start()
        passes.append(copy)

    def part_copy(d, c):
        return pltpu.make_async_remote_copy(
            src_ref=sent.at[d - 1, c],
            dst_ref=landed.at[d - 1, c],
            send_sem=p_send.at[d, c],
            recv_sem=p_recv.at[d, c],
            device_id=behind[d],
            device_id_type=MESH,
        )

    for d in range(1, owners):
        passes[d - 1].wait_recv()

        @pl.loop(0, chunks)
        def _(c):
            for m in range(2):
                sent[d - 1, c, :, m * piece : (m + 1) * piece] = product(d, c, m).astype(sent.dtype)
            part_copy(d, c).start()

    tile = min(depth, 256)
    for d in range(owners):

        @pl.loop(0, depth // tile)
        def _(i):
            span = pl.ds(pl.multiple_of(i * tile, tile), tile)
            flipped[span, d * rows : (d + 1) * rows] = x_all[d, :, span].T

    turned_out = pltpu.make_async_copy(flipped, turned, out_sems.at[0])
    turned_out.start()

    def delta_copy(d, c):
        return pltpu.make_async_remote_copy(
            src_ref=delta_all.at[c, pl.ds(0, rows), :],
            dst_ref=delta_all.at[c, pl.ds(d * rows, rows), :],
            send_sem=d_send.at[d, c],
            recv_sem=d_recv.at[d, c],
            device_id=ahead[d],
            device_id_type=MESH,
        )

    @pl.loop(0, chunks)
    def _(c):
        for d in range(1, owners):
            part_copy(d, c).wait_recv()
        cols = pl.ds(pl.multiple_of(c * piece, piece), piece)
        gate = own[c, :, 0:piece]
        up = own[c, :, piece:pair]
        for d in range(1, owners):
            gate = gate + landed[d - 1, c, :, 0:piece].astype(jnp.float32)
            up = up + landed[d - 1, c, :, piece:pair].astype(jnp.float32)
        sigmoid = jax.nn.sigmoid(gate)
        silu = gate * sigmoid
        hidden_all[:, cols] = (silu * up).astype(hidden_all.dtype)
        cot = cotangent[:, cols].astype(jnp.float32)
        gate_delta = cot * up * sigmoid * (1.0 + gate * (1.0 - sigmoid))
        delta_all[c, 0:rows, 0:piece] = gate_delta.astype(delta_all.dtype)
        delta_all[c, 0:rows, piece:pair] = (cot * silu).astype(delta_all.dtype)
        for d in range(1, owners):
            delta_copy(d, c).start()

    hidden_out = pltpu.make_async_copy(hidden_all, hidden, out_sems.at[1])
    hidden_out.start()

    @pl.loop(0, chunks)
    def _(c):
        for d in range(1, owners):
            delta_copy(d, c).wait_recv()
        pltpu.make_async_copy(delta_all.at[c], delta.at[c], w_sems.at[c, 0]).start()

    for copy in x_copies + passes:
        copy.wait_send()

    @pl.loop(0, chunks)
    def _(c):
        for d in range(1, owners):
            part_copy(d, c).wait_send()
            delta_copy(d, c).wait_send()
        pltpu.make_async_copy(delta_all.at[c], delta.at[c], w_sems.at[c, 0]).wait()

    turned_out.wait()
    hidden_out.wait()


def exchange(features, placed, cotangent, owners):
    rows, width = cotangent.shape
    depth = placed.shape[0]
    piece = min(width, 512)
    chunks = width // piece
    everyone = owners * rows
    dma = pltpu.SemaphoreType.DMA
    return pl.pallas_call(
        exchange_kernel,
        out_shape=(
            jax.ShapeDtypeStruct((rows, width), jnp.bfloat16),
            jax.ShapeDtypeStruct((depth, everyone), jnp.bfloat16),
            jax.ShapeDtypeStruct((chunks, everyone, 2 * piece), jnp.bfloat16),
        ),
        in_specs=[
            pl.BlockSpec(memory_space=pl.ANY),
            pl.BlockSpec(memory_space=pl.ANY),
            pl.BlockSpec(memory_space=pltpu.VMEM),
        ],
        out_specs=(pl.BlockSpec(memory_space=pl.ANY),) * 3,
        scratch_shapes=[
            pltpu.VMEM((depth, 2 * width), jnp.bfloat16),
            pltpu.VMEM((owners, rows, depth), jnp.bfloat16),
            pltpu.VMEM((depth, everyone), jnp.bfloat16),
            pltpu.VMEM((chunks, rows, 2 * piece), jnp.float32),
            pltpu.VMEM((owners - 1, chunks, rows, 2 * piece), jnp.bfloat16),
            pltpu.VMEM((owners - 1, chunks, rows, 2 * piece), jnp.bfloat16),
            pltpu.VMEM((chunks, everyone, 2 * piece), jnp.bfloat16),
            pltpu.VMEM((rows, width), jnp.bfloat16),
            dma((chunks, 2)),
            dma((owners,)),
            dma((owners,)),
            dma((owners,)),
            dma((owners,)),
            dma((owners, chunks)),
            dma((owners, chunks)),
            dma((owners, chunks)),
            dma((owners, chunks)),
            dma((2,)),
        ],
        compiler_params=pltpu.CompilerParams(
            collective_id=0, has_side_effects=True, vmem_limit_bytes=56 << 20
        ),
        cost_estimate=pl.CostEstimate(
            flops=4 * everyone * depth * width,
            bytes_accessed=4 * depth * width,
            transcendentals=rows * width,
        ),
    )(features, placed, cotangent)


def grad_kernel(lists, counts, turned, delta, gate_grad, up_grad, dense, sems):
    capacity, block, _ = gate_grad.shape
    depth = turned.shape[0]
    chunks, _, pair = delta.shape
    piece = pair // 2
    width = chunks * piece
    cols = width // block
    strip = min(depth, 256)
    outs = (gate_grad, up_grad)
    for m, out in enumerate(outs):
        dense[m, depth : depth + block, 0:block] = jnp.zeros((block, block), dense.dtype)

        @pl.loop(0, depth // strip)
        def _(i):
            rows = pl.ds(pl.multiple_of(i * strip, strip), strip)
            for c in range(chunks):
                dense[m, rows, c * piece : (c + 1) * piece] = jnp.dot(
                    turned[rows, :],
                    delta[c, :, m * piece : (m + 1) * piece],
                    preferred_element_type=jnp.float32,
                ).astype(dense.dtype)

        @pl.loop(0, capacity)
        def _(k):
            position = lists[m, k]
            live = k < counts[m]
            row = jnp.where(live, lax.div(position, cols) * block, depth)
            col = jnp.where(live, lax.rem(position, cols) * block, 0)
            source = dense.at[
                m, pl.ds(pl.multiple_of(row, block), block), pl.ds(pl.multiple_of(col, block), block)
            ]
            pltpu.make_async_copy(source, out.at[k], sems.at[m]).start()

    for m, out in enumerate(outs):
        pltpu.make_async_copy(out, out, sems.at[m]).wait()


def block_grads(lists, counts, turned, delta, capacity, block):
    depth = turned.shape[0]
    width = delta.shape[0] * delta.shape[2] // 2
    shape = jax.ShapeDtypeStruct((capacity, block, block), jnp.bfloat16)
    return pl.pallas_call(
        grad_kernel,
        out_shape=(shape, shape),
        in_specs=[
            pl.BlockSpec(memory_space=pltpu.SMEM),
            pl.BlockSpec(memory_space=pltpu.SMEM),
            pl.BlockSpec(memory_space=pltpu.VMEM),
            pl.BlockSpec(memory_space=pltpu.VMEM),
        ],
        out_specs=(pl.BlockSpec(memory_space=pl.ANY), pl.BlockSpec(memory_space=pl.ANY)),
        scratch_shapes=[
            pltpu.VMEM((2, depth + block, width), jnp.bfloat16),
            pltpu.SemaphoreType.DMA((2,)),
        ],
        compiler_params=pltpu.CompilerParams(vmem_limit_bytes=56 << 20),
        cost_estimate=pl.CostEstimate(
            flops=4 * depth * width * turned.shape[1],
            bytes_accessed=4 * capacity * block * block,
            transcendentals=0,
        ),
    )(lists, counts, turned, delta)


def shards(tokens, gate_blocks, up_blocks, gate_list, gate_count, up_list, up_count, cotangent):
    owners = lax.axis_size("token")
    me = lax.axis_index("token")
    capacity, block = gate_blocks.shape[2:4]
    width = cotangent.shape[1]
    model = tokens.shape[1] * lax.axis_size("weight") * lax.axis_size("sub")
    depth = model // owners
    lists = jnp.stack([gate_list[me, 0], up_list[me, 0]])
    counts = jnp.stack([gate_count[me, 0], up_count[me, 0]])

    features = lax.all_gather(tokens, ("weight", "sub"), axis=1, tiled=True)
    placed = place(lists, counts, gate_blocks[0, 0], up_blocks[0, 0], depth, width)
    hidden, turned, delta = exchange(features, placed, cotangent, owners)
    gate_grad, up_grad = block_grads(lists, counts, turned, delta, capacity, block)
    shape = (1, 1, capacity, block, block)
    return (hidden, gate_grad.reshape(shape), up_grad.reshape(shape))


def solution(mesh):
    return jax.shard_map(
        shards,
        mesh=mesh,
        in_specs=(
            P(("groups", "token"), ("weight", "sub")),
            P("token", ("weight", "sub"), None, None, None),
            P("token", ("weight", "sub"), None, None, None),
            P(None, ("weight", "sub"), None),
            P(None, ("weight", "sub")),
            P(None, ("weight", "sub"), None),
            P(None, ("weight", "sub")),
            P(("groups", "token"), ("weight", "sub")),
        ),
        out_specs=(
            P(("groups", "token"), ("weight", "sub")),
            P(("groups", "token"), ("weight", "sub"), None, None, None),
            P(("groups", "token"), ("weight", "sub"), None, None, None),
        ),
        check_vma=False,
    )
```

```python
import jax
import jax.numpy as jnp
from jax import lax
from jax.experimental import pallas as pl
from jax.experimental.pallas import tpu as pltpu
from jax.sharding import PartitionSpec as P

MESH = pl.DeviceIdType.MESH


def place_kernel(
    lists, counts, gate_blocks, up_blocks, placed, dense, held, block_sems, out_sems
):
    capacity, block, _ = gate_blocks.shape
    depth, both = dense.shape
    width = both // 2
    cols = width // block
    strip = min(depth, 256)
    sources = (gate_blocks, up_blocks)
    reads, writes = [], []
    for m, source in enumerate(sources):
        read = pltpu.make_async_copy(source, held.at[m], block_sems.at[m])
        read.start()
        reads.append(read)
    for m in range(2):

        @pl.loop(0, depth // strip)
        def _(i):
            rows = pl.ds(pl.multiple_of(i * strip, strip), strip)
            dense[rows, m * width : (m + 1) * width] = jnp.zeros((strip, width), dense.dtype)

        reads[m].wait()

        @pl.loop(0, capacity, unroll=8)
        def _(k):
            position = lists[m, k]
            row = pl.multiple_of(lax.div(position, cols) * block, block)
            col = pl.multiple_of(m * width + lax.rem(position, cols) * block, block)
            kept = jnp.where(k < counts[m], held[m, k], jnp.zeros((block, block), dense.dtype))
            dense[pl.ds(row, block), pl.ds(col, block)] = kept

        half = pl.ds(m * width, width)
        write = pltpu.make_async_copy(dense.at[:, half], placed.at[:, half], out_sems.at[m])
        write.start()
        writes.append(write)
    for write in writes:
        write.wait()


def place(lists, counts, gate_blocks, up_blocks, depth, width):
    return pl.pallas_call(
        place_kernel,
        out_shape=jax.ShapeDtypeStruct((depth, 2 * width), gate_blocks.dtype),
        in_specs=[
            pl.BlockSpec(memory_space=pltpu.SMEM),
            pl.BlockSpec(memory_space=pltpu.SMEM),
            pl.BlockSpec(memory_space=pl.ANY),
            pl.BlockSpec(memory_space=pl.ANY),
        ],
        out_specs=pl.BlockSpec(memory_space=pl.ANY),
        scratch_shapes=[
            pltpu.VMEM((depth, 2 * width), gate_blocks.dtype),
            pltpu.VMEM((2, *gate_blocks.shape), gate_blocks.dtype),
            pltpu.SemaphoreType.DMA((2,)),
            pltpu.SemaphoreType.DMA((2,)),
        ],
        compiler_params=pltpu.CompilerParams(vmem_limit_bytes=60 << 20),
        cost_estimate=pl.CostEstimate(
            flops=0, bytes_accessed=2 * gate_blocks.size * 2 + depth * width * 4, transcendentals=0
        ),
    )(lists, counts, gate_blocks, up_blocks)


def exchange_kernel(
    features, placed, cotangent, hidden, turned, delta,
    weights, x_all, flipped, own, sent, landed, delta_all, hidden_all,
    w_sems, mine_sems, x_send, x_recv, pass_send, pass_recv, p_send, p_recv, d_send, d_recv, out_sems,
):
    owners = lax.axis_size("token")
    me = lax.axis_index("token")
    sub = lax.axis_index("sub")
    rows, depth = x_all.shape[1:]
    chunks, _, pair = delta_all.shape
    piece = pair // 2
    width = chunks * piece
    local = features.shape[2]
    subs = lax.axis_size("sub")
    shares = depth // (local * subs)
    sibling = {"sub": 1 - sub}
    ahead = [{"token": lax.rem(me + d, owners)} for d in range(owners)]
    behind = [{"token": lax.rem(me + owners - d, owners)} for d in range(owners)]

    barrier = pltpu.get_barrier_semaphore()
    for d in range(1, owners):
        pl.semaphore_signal(barrier, inc=1, device_id=ahead[d], device_id_type=MESH)
    pl.semaphore_signal(barrier, inc=1, device_id=sibling, device_id_type=MESH)

    def weight_copy(c, m):
        cols = pl.ds(pl.multiple_of(m * width + c * piece, piece), piece)
        return pltpu.make_async_copy(placed.at[:, cols], weights.at[:, cols], w_sems.at[c, m])

    def share(i):
        return pl.ds(pl.multiple_of((i * subs + sub) * local, local), local)

    mine = [
        pltpu.make_async_copy(
            features.at[me * shares + i], x_all.at[0, :, share(i)], mine_sems.at[i]
        )
        for i in range(shares)
    ]
    for copy in mine:
        copy.start()
    for m in range(2):
        weight_copy(0, m).start()
    pl.semaphore_wait(barrier, owners)

    x_copies = []
    for d in range(1, owners):
        first = lax.rem(me + d, owners) * shares
        for i in range(shares):
            copy = pltpu.make_async_remote_copy(
                src_ref=features.at[first + i],
                dst_ref=x_all.at[d, :, share(i)],
                send_sem=x_send.at[d, i],
                recv_sem=x_recv.at[d, i],
                device_id=ahead[d],
                device_id_type=MESH,
            )
            copy.start()
            x_copies.append(copy)

    passes = []
    for i in range(shares):
        copy = pltpu.make_async_remote_copy(
            src_ref=features.at[me * shares + i],
            dst_ref=x_all.at[0, :, share(i)],
            send_sem=pass_send.at[0, i],
            recv_sem=pass_recv.at[0, i],
            device_id=sibling,
            device_id_type=MESH,
        )
        copy.start()
        passes.append(copy)

    @pl.loop(1, chunks)
    def _(c):
        for m in range(2):
            weight_copy(c, m).start()

    for copy in mine:
        copy.wait()
    for copy in passes:
        copy.wait_recv()

    def product(slot, c, m):
        cols = pl.ds(pl.multiple_of(m * width + c * piece, piece), piece)
        return jnp.dot(x_all[slot], weights[:, cols], preferred_element_type=jnp.float32)

    @pl.loop(0, chunks)
    def _(c):
        for m in range(2):
            weight_copy(c, m).wait()
            own[c, :, m * piece : (m + 1) * piece] = product(0, c, m)

    for d in range(1, owners):
        for i in range(shares):
            x_copies[(d - 1) * shares + i].wait_recv()
            copy = pltpu.make_async_remote_copy(
                src_ref=x_all.at[d, :, share(i)],
                dst_ref=x_all.at[d, :, share(i)],
                send_sem=pass_send.at[d, i],
                recv_sem=pass_recv.at[d, i],
                device_id=sibling,
                device_id_type=MESH,
            )
            copy.start()
            passes.append(copy)

    def part_copy(d, c):
        return pltpu.make_async_remote_copy(
            src_ref=sent.at[d - 1, c],
            dst_ref=landed.at[d - 1, c],
            send_sem=p_send.at[d, c],
            recv_sem=p_recv.at[d, c],
            device_id=behind[d],
            device_id_type=MESH,
        )

    for d in range(1, owners):
        for i in range(shares):
            passes[d * shares + i].wait_recv()

        @pl.loop(0, chunks)
        def _(c):
            for m in range(2):
                sent[d - 1, c, :, m * piece : (m + 1) * piece] = product(d, c, m).astype(sent.dtype)
            part_copy(d, c).start()

    tile = min(depth, 256)
    for d in range(owners):

        @pl.loop(0, depth // tile)
        def _(i):
            span = pl.ds(pl.multiple_of(i * tile, tile), tile)
            flipped[span, d * rows : (d + 1) * rows] = x_all[d, :, span].T

    turned_out = pltpu.make_async_copy(flipped, turned, out_sems.at[0])
    turned_out.start()

    def delta_copy(d, c):
        return pltpu.make_async_remote_copy(
            src_ref=delta_all.at[c, pl.ds(0, rows), :],
            dst_ref=delta_all.at[c, pl.ds(d * rows, rows), :],
            send_sem=d_send.at[d, c],
            recv_sem=d_recv.at[d, c],
            device_id=ahead[d],
            device_id_type=MESH,
        )

    @pl.loop(0, chunks)
    def _(c):
        for d in range(1, owners):
            part_copy(d, c).wait_recv()
        cols = pl.ds(pl.multiple_of(c * piece, piece), piece)
        gate = own[c, :, 0:piece]
        up = own[c, :, piece:pair]
        for d in range(1, owners):
            gate = gate + landed[d - 1, c, :, 0:piece].astype(jnp.float32)
            up = up + landed[d - 1, c, :, piece:pair].astype(jnp.float32)
        sigmoid = jax.nn.sigmoid(gate)
        silu = gate * sigmoid
        hidden_all[:, cols] = (silu * up).astype(hidden_all.dtype)
        cot = cotangent[:, cols].astype(jnp.float32)
        gate_delta = cot * up * sigmoid * (1.0 + gate * (1.0 - sigmoid))
        delta_all[c, 0:rows, 0:piece] = gate_delta.astype(delta_all.dtype)
        delta_all[c, 0:rows, piece:pair] = (cot * silu).astype(delta_all.dtype)
        for d in range(1, owners):
            delta_copy(d, c).start()

    hidden_out = pltpu.make_async_copy(hidden_all, hidden, out_sems.at[1])
    hidden_out.start()

    @pl.loop(0, chunks)
    def _(c):
        for d in range(1, owners):
            delta_copy(d, c).wait_recv()
        pltpu.make_async_copy(delta_all.at[c], delta.at[c], w_sems.at[c, 0]).start()

    for copy in x_copies + passes:
        copy.wait_send()

    @pl.loop(0, chunks)
    def _(c):
        for d in range(1, owners):
            part_copy(d, c).wait_send()
            delta_copy(d, c).wait_send()
        pltpu.make_async_copy(delta_all.at[c], delta.at[c], w_sems.at[c, 0]).wait()

    turned_out.wait()
    hidden_out.wait()


def exchange(features, placed, cotangent, owners):
    rows, width = cotangent.shape
    depth = placed.shape[0]
    piece = min(width, 512)
    chunks = width // piece
    shares = features.shape[0] // owners
    everyone = owners * rows
    dma = pltpu.SemaphoreType.DMA
    return pl.pallas_call(
        exchange_kernel,
        out_shape=(
            jax.ShapeDtypeStruct((rows, width), jnp.bfloat16),
            jax.ShapeDtypeStruct((depth, everyone), jnp.bfloat16),
            jax.ShapeDtypeStruct((chunks, everyone, 2 * piece), jnp.bfloat16),
        ),
        in_specs=[
            pl.BlockSpec(memory_space=pl.ANY),
            pl.BlockSpec(memory_space=pl.ANY),
            pl.BlockSpec(memory_space=pltpu.VMEM),
        ],
        out_specs=(pl.BlockSpec(memory_space=pl.ANY),) * 3,
        scratch_shapes=[
            pltpu.VMEM((depth, 2 * width), jnp.bfloat16),
            pltpu.VMEM((owners, rows, depth), jnp.bfloat16),
            pltpu.VMEM((depth, everyone), jnp.bfloat16),
            pltpu.VMEM((chunks, rows, 2 * piece), jnp.float32),
            pltpu.VMEM((owners - 1, chunks, rows, 2 * piece), jnp.bfloat16),
            pltpu.VMEM((owners - 1, chunks, rows, 2 * piece), jnp.bfloat16),
            pltpu.VMEM((chunks, everyone, 2 * piece), jnp.bfloat16),
            pltpu.VMEM((rows, width), jnp.bfloat16),
            dma((chunks, 2)),
            dma((shares,)),
            dma((owners, shares)),
            dma((owners, shares)),
            dma((owners, shares)),
            dma((owners, shares)),
            dma((owners, chunks)),
            dma((owners, chunks)),
            dma((owners, chunks)),
            dma((owners, chunks)),
            dma((2,)),
        ],
        compiler_params=pltpu.CompilerParams(
            collective_id=0, has_side_effects=True, vmem_limit_bytes=56 << 20
        ),
        cost_estimate=pl.CostEstimate(
            flops=4 * everyone * depth * width,
            bytes_accessed=4 * depth * width,
            transcendentals=rows * width,
        ),
    )(features, placed, cotangent)


def grad_kernel(lists, counts, turned, delta, gate_grad, up_grad, dense, staged, sems):
    capacity, block, _ = gate_grad.shape
    depth = turned.shape[0]
    chunks, _, pair = delta.shape
    piece = pair // 2
    width = chunks * piece
    cols = width // block
    positions = dense.shape[0] - 1
    strip = min(depth, 512)
    groups = sems.shape[1]
    group = capacity // groups
    outs = (gate_grad, up_grad)
    dense[positions] = jnp.zeros((block, block), dense.dtype)
    writes = []
    for m, out in enumerate(outs):

        @pl.loop(0, depth // strip)
        def _(i):
            rows = pl.ds(pl.multiple_of(i * strip, strip), strip)
            for c in range(chunks):
                term = jnp.dot(
                    turned[rows, :],
                    delta[c, :, m * piece : (m + 1) * piece],
                    preferred_element_type=jnp.float32,
                ).astype(dense.dtype)
                for r in range(strip // block):
                    for q in range(piece // block):
                        place_at = (i * (strip // block) + r) * cols + c * (piece // block) + q
                        dense[place_at] = term[
                            r * block : (r + 1) * block, q * block : (q + 1) * block
                        ]

        for g in range(groups):

            @pl.loop(0, group, unroll=8)
            def _(j):
                k = g * group + j
                staged[m, k] = dense[jnp.where(k < counts[m], lists[m, k], positions)]

            span = pl.ds(g * group, group)
            write = pltpu.make_async_copy(staged.at[m, span], out.at[span], sems.at[m, g])
            write.start()
            writes.append(write)
    for write in writes:
        write.wait()


def block_grads(lists, counts, turned, delta, capacity, block):
    depth = turned.shape[0]
    width = delta.shape[0] * delta.shape[2] // 2
    shape = jax.ShapeDtypeStruct((capacity, block, block), jnp.bfloat16)
    return pl.pallas_call(
        grad_kernel,
        out_shape=(shape, shape),
        in_specs=[
            pl.BlockSpec(memory_space=pltpu.SMEM),
            pl.BlockSpec(memory_space=pltpu.SMEM),
            pl.BlockSpec(memory_space=pltpu.VMEM),
            pl.BlockSpec(memory_space=pltpu.VMEM),
        ],
        out_specs=(pl.BlockSpec(memory_space=pl.ANY), pl.BlockSpec(memory_space=pl.ANY)),
        scratch_shapes=[
            pltpu.VMEM((depth * width // block**2 + 1, block, block), jnp.bfloat16),
            pltpu.VMEM((2, capacity, block, block), jnp.bfloat16),
            pltpu.SemaphoreType.DMA((2, 4 if capacity % 32 == 0 else 1)),
        ],
        compiler_params=pltpu.CompilerParams(vmem_limit_bytes=56 << 20),
        cost_estimate=pl.CostEstimate(
            flops=4 * depth * width * turned.shape[1],
            bytes_accessed=4 * capacity * block * block,
            transcendentals=0,
        ),
    )(lists, counts, turned, delta)


def shards(tokens, gate_blocks, up_blocks, gate_list, gate_count, up_list, up_count, cotangent):
    owners = lax.axis_size("token")
    me = lax.axis_index("token")
    capacity, block = gate_blocks.shape[2:4]
    width = cotangent.shape[1]
    model = tokens.shape[1] * lax.axis_size("weight") * lax.axis_size("sub")
    depth = model // owners
    lists = jnp.stack([gate_list[me, 0], up_list[me, 0]])
    counts = jnp.stack([gate_count[me, 0], up_count[me, 0]])

    features = lax.all_gather(tokens, "weight", axis=0)
    placed = place(lists, counts, gate_blocks[0, 0], up_blocks[0, 0], depth, width)
    hidden, turned, delta = exchange(features, placed, cotangent, owners)
    gate_grad, up_grad = block_grads(lists, counts, turned, delta, capacity, block)
    shape = (1, 1, capacity, block, block)
    return (hidden, gate_grad.reshape(shape), up_grad.reshape(shape))


def solution(mesh):
    return jax.shard_map(
        shards,
        mesh=mesh,
        in_specs=(
            P(("groups", "token"), ("weight", "sub")),
            P("token", ("weight", "sub"), None, None, None),
            P("token", ("weight", "sub"), None, None, None),
            P(None, ("weight", "sub"), None),
            P(None, ("weight", "sub")),
            P(None, ("weight", "sub"), None),
            P(None, ("weight", "sub")),
            P(("groups", "token"), ("weight", "sub")),
        ),
        out_specs=(
            P(("groups", "token"), ("weight", "sub")),
            P(("groups", "token"), ("weight", "sub"), None, None, None),
            P(("groups", "token"), ("weight", "sub"), None, None, None),
        ),
        check_vma=False,
    )
```

```python
import jax
import jax.numpy as jnp
from jax import lax
from jax.experimental import pallas as pl
from jax.experimental.pallas import tpu as pltpu
from jax.sharding import PartitionSpec as P

MESH = pl.DeviceIdType.MESH


def place_kernel(
    lists, counts, gate_blocks, up_blocks, placed, dense, held, block_sems, out_sems
):
    capacity, block, _ = gate_blocks.shape
    depth, both = dense.shape
    width = both // 2
    cols = width // block
    strip = min(depth, 256)
    sources = (gate_blocks, up_blocks)
    reads, writes = [], []
    for m, source in enumerate(sources):
        read = pltpu.make_async_copy(source, held.at[m], block_sems.at[m])
        read.start()
        reads.append(read)
    for m in range(2):

        @pl.loop(0, depth // strip)
        def _(i):
            rows = pl.ds(pl.multiple_of(i * strip, strip), strip)
            dense[rows, m * width : (m + 1) * width] = jnp.zeros((strip, width), dense.dtype)

        reads[m].wait()

        @pl.loop(0, capacity, unroll=8)
        def _(k):
            position = lists[m, k]
            row = pl.multiple_of(lax.div(position, cols) * block, block)
            col = pl.multiple_of(m * width + lax.rem(position, cols) * block, block)
            kept = jnp.where(k < counts[m], held[m, k], jnp.zeros((block, block), dense.dtype))
            dense[pl.ds(row, block), pl.ds(col, block)] = kept

        half = pl.ds(m * width, width)
        write = pltpu.make_async_copy(dense.at[:, half], placed.at[:, half], out_sems.at[m])
        write.start()
        writes.append(write)
    for write in writes:
        write.wait()


def place(lists, counts, gate_blocks, up_blocks, depth, width):
    return pl.pallas_call(
        place_kernel,
        out_shape=jax.ShapeDtypeStruct((depth, 2 * width), gate_blocks.dtype),
        in_specs=[
            pl.BlockSpec(memory_space=pltpu.SMEM),
            pl.BlockSpec(memory_space=pltpu.SMEM),
            pl.BlockSpec(memory_space=pl.ANY),
            pl.BlockSpec(memory_space=pl.ANY),
        ],
        out_specs=pl.BlockSpec(memory_space=pl.ANY),
        scratch_shapes=[
            pltpu.VMEM((depth, 2 * width), gate_blocks.dtype),
            pltpu.VMEM((2, *gate_blocks.shape), gate_blocks.dtype),
            pltpu.SemaphoreType.DMA((2,)),
            pltpu.SemaphoreType.DMA((2,)),
        ],
        compiler_params=pltpu.CompilerParams(vmem_limit_bytes=60 << 20),
        cost_estimate=pl.CostEstimate(
            flops=0, bytes_accessed=2 * gate_blocks.size * 2 + depth * width * 4, transcendentals=0
        ),
    )(lists, counts, gate_blocks, up_blocks)


def exchange_kernel(
    features, placed, cotangent, hidden, turned, delta,
    weights, x_all, flipped, own, sent, landed, delta_all, hidden_all,
    w_sems, mine_sems, pass_send, pass_recv, p_send, p_recv, d_send, d_recv, out_sems,
):
    owners = lax.axis_size("token")
    me = lax.axis_index("token")
    sub = lax.axis_index("sub")
    rows, depth = x_all.shape[1:]
    chunks, _, pair = delta_all.shape
    piece = pair // 2
    width = chunks * piece
    local = features.shape[2]
    subs = lax.axis_size("sub")
    shares = depth // (local * subs)
    sibling = {"sub": 1 - sub}
    ahead = [{"token": lax.rem(me + d, owners)} for d in range(owners)]
    behind = [{"token": lax.rem(me + owners - d, owners)} for d in range(owners)]

    barrier = pltpu.get_barrier_semaphore()
    for d in range(1, owners):
        pl.semaphore_signal(barrier, inc=1, device_id=ahead[d], device_id_type=MESH)
    pl.semaphore_signal(barrier, inc=1, device_id=sibling, device_id_type=MESH)

    def weight_copy(c, m):
        cols = pl.ds(pl.multiple_of(m * width + c * piece, piece), piece)
        return pltpu.make_async_copy(placed.at[:, cols], weights.at[:, cols], w_sems.at[c, m])

    def share(i):
        return pl.ds(pl.multiple_of((i * subs + sub) * local, local), local)

    def held_share(d, i):
        group = lax.rem(me + owners - d, owners)
        return features.at[group * (shares * owners) + me * shares + i]

    mine = [
        pltpu.make_async_copy(held_share(d, i), x_all.at[d, :, share(i)], mine_sems.at[d, i])
        for d in range(owners)
        for i in range(shares)
    ]
    for copy in mine:
        copy.start()
    for m in range(2):
        weight_copy(0, m).start()
    pl.semaphore_wait(barrier, owners)

    passes = [
        pltpu.make_async_remote_copy(
            src_ref=held_share(d, i),
            dst_ref=x_all.at[d, :, share(i)],
            send_sem=pass_send.at[d, i],
            recv_sem=pass_recv.at[d, i],
            device_id=sibling,
            device_id_type=MESH,
        )
        for d in range(owners)
        for i in range(shares)
    ]
    for copy in passes:
        copy.start()

    @pl.loop(1, chunks)
    def _(c):
        for m in range(2):
            weight_copy(c, m).start()

    for copy in mine:
        copy.wait()
    for copy in passes:
        copy.wait_recv()

    def product(slot, c, m):
        cols = pl.ds(pl.multiple_of(m * width + c * piece, piece), piece)
        return jnp.dot(x_all[slot], weights[:, cols], preferred_element_type=jnp.float32)

    def part_copy(d, c):
        return pltpu.make_async_remote_copy(
            src_ref=sent.at[d - 1, c],
            dst_ref=landed.at[d - 1, c],
            send_sem=p_send.at[d, c],
            recv_sem=p_recv.at[d, c],
            device_id=behind[d],
            device_id_type=MESH,
        )

    @pl.loop(0, chunks)
    def _(c):
        for m in range(2):
            weight_copy(c, m).wait()
        for d in range(1, owners):
            for m in range(2):
                sent[d - 1, c, :, m * piece : (m + 1) * piece] = product(d, c, m).astype(sent.dtype)
            part_copy(d, c).start()
        for m in range(2):
            own[c, :, m * piece : (m + 1) * piece] = product(0, c, m)

    tile = min(depth, 256)
    for d in range(owners):

        @pl.loop(0, depth // tile)
        def _(i):
            span = pl.ds(pl.multiple_of(i * tile, tile), tile)
            flipped[span, d * rows : (d + 1) * rows] = x_all[d, :, span].T

    turned_out = pltpu.make_async_copy(flipped, turned, out_sems.at[0])
    turned_out.start()

    def delta_copy(d, c):
        return pltpu.make_async_remote_copy(
            src_ref=delta_all.at[c, pl.ds(0, rows), :],
            dst_ref=delta_all.at[c, pl.ds(d * rows, rows), :],
            send_sem=d_send.at[d, c],
            recv_sem=d_recv.at[d, c],
            device_id=ahead[d],
            device_id_type=MESH,
        )

    @pl.loop(0, chunks)
    def _(c):
        for d in range(1, owners):
            part_copy(d, c).wait_recv()
        cols = pl.ds(pl.multiple_of(c * piece, piece), piece)
        gate = own[c, :, 0:piece]
        up = own[c, :, piece:pair]
        for d in range(1, owners):
            gate = gate + landed[d - 1, c, :, 0:piece].astype(jnp.float32)
            up = up + landed[d - 1, c, :, piece:pair].astype(jnp.float32)
        sigmoid = jax.nn.sigmoid(gate)
        silu = gate * sigmoid
        hidden_all[:, cols] = (silu * up).astype(hidden_all.dtype)
        cot = cotangent[:, cols].astype(jnp.float32)
        gate_delta = cot * up * sigmoid * (1.0 + gate * (1.0 - sigmoid))
        delta_all[c, 0:rows, 0:piece] = gate_delta.astype(delta_all.dtype)
        delta_all[c, 0:rows, piece:pair] = (cot * silu).astype(delta_all.dtype)
        for d in range(1, owners):
            delta_copy(d, c).start()

    hidden_out = pltpu.make_async_copy(hidden_all, hidden, out_sems.at[1])
    hidden_out.start()

    @pl.loop(0, chunks)
    def _(c):
        for d in range(1, owners):
            delta_copy(d, c).wait_recv()
        pltpu.make_async_copy(delta_all.at[c], delta.at[c], w_sems.at[c, 0]).start()

    for copy in passes:
        copy.wait_send()

    @pl.loop(0, chunks)
    def _(c):
        for d in range(1, owners):
            part_copy(d, c).wait_send()
            delta_copy(d, c).wait_send()
        pltpu.make_async_copy(delta_all.at[c], delta.at[c], w_sems.at[c, 0]).wait()

    turned_out.wait()
    hidden_out.wait()


def exchange(features, placed, cotangent, owners):
    rows, width = cotangent.shape
    depth = placed.shape[0]
    piece = min(width, 512)
    chunks = width // piece
    shares = features.shape[0] // owners**2
    everyone = owners * rows
    dma = pltpu.SemaphoreType.DMA
    return pl.pallas_call(
        exchange_kernel,
        out_shape=(
            jax.ShapeDtypeStruct((rows, width), jnp.bfloat16),
            jax.ShapeDtypeStruct((depth, everyone), jnp.bfloat16),
            jax.ShapeDtypeStruct((chunks, everyone, 2 * piece), jnp.bfloat16),
        ),
        in_specs=[
            pl.BlockSpec(memory_space=pl.ANY),
            pl.BlockSpec(memory_space=pl.ANY),
            pl.BlockSpec(memory_space=pltpu.VMEM),
        ],
        out_specs=(pl.BlockSpec(memory_space=pl.ANY),) * 3,
        scratch_shapes=[
            pltpu.VMEM((depth, 2 * width), jnp.bfloat16),
            pltpu.VMEM((owners, rows, depth), jnp.bfloat16),
            pltpu.VMEM((depth, everyone), jnp.bfloat16),
            pltpu.VMEM((chunks, rows, 2 * piece), jnp.float32),
            pltpu.VMEM((owners - 1, chunks, rows, 2 * piece), jnp.bfloat16),
            pltpu.VMEM((owners - 1, chunks, rows, 2 * piece), jnp.bfloat16),
            pltpu.VMEM((chunks, everyone, 2 * piece), jnp.bfloat16),
            pltpu.VMEM((rows, width), jnp.bfloat16),
            dma((chunks, 2)),
            dma((owners, shares)),
            dma((owners, shares)),
            dma((owners, shares)),
            dma((owners, chunks)),
            dma((owners, chunks)),
            dma((owners, chunks)),
            dma((owners, chunks)),
            dma((2,)),
        ],
        compiler_params=pltpu.CompilerParams(
            collective_id=0, has_side_effects=True, vmem_limit_bytes=56 << 20
        ),
        cost_estimate=pl.CostEstimate(
            flops=4 * everyone * depth * width,
            bytes_accessed=4 * depth * width,
            transcendentals=rows * width,
        ),
    )(features, placed, cotangent)


def grad_kernel(lists, counts, turned, delta, gate_grad, up_grad, dense, staged, sems):
    capacity, block, _ = gate_grad.shape
    depth = turned.shape[0]
    chunks, _, pair = delta.shape
    piece = pair // 2
    width = chunks * piece
    cols = width // block
    positions = dense.shape[0] - 1
    strip = min(depth, 512)
    groups = sems.shape[1]
    group = capacity // groups
    outs = (gate_grad, up_grad)
    dense[positions] = jnp.zeros((block, block), dense.dtype)
    writes = []
    for m, out in enumerate(outs):

        @pl.loop(0, depth // strip)
        def _(i):
            rows = pl.ds(pl.multiple_of(i * strip, strip), strip)
            for c in range(chunks):
                term = jnp.dot(
                    turned[rows, :],
                    delta[c, :, m * piece : (m + 1) * piece],
                    preferred_element_type=jnp.float32,
                ).astype(dense.dtype)
                for r in range(strip // block):
                    for q in range(piece // block):
                        place_at = (i * (strip // block) + r) * cols + c * (piece // block) + q
                        dense[place_at] = term[
                            r * block : (r + 1) * block, q * block : (q + 1) * block
                        ]

        for g in range(groups):

            @pl.loop(0, group, unroll=8)
            def _(j):
                k = g * group + j
                staged[m, k] = dense[jnp.where(k < counts[m], lists[m, k], positions)]

            span = pl.ds(g * group, group)
            write = pltpu.make_async_copy(staged.at[m, span], out.at[span], sems.at[m, g])
            write.start()
            writes.append(write)
    for write in writes:
        write.wait()


def block_grads(lists, counts, turned, delta, capacity, block):
    depth = turned.shape[0]
    width = delta.shape[0] * delta.shape[2] // 2
    shape = jax.ShapeDtypeStruct((capacity, block, block), jnp.bfloat16)
    return pl.pallas_call(
        grad_kernel,
        out_shape=(shape, shape),
        in_specs=[
            pl.BlockSpec(memory_space=pltpu.SMEM),
            pl.BlockSpec(memory_space=pltpu.SMEM),
            pl.BlockSpec(memory_space=pltpu.VMEM),
            pl.BlockSpec(memory_space=pltpu.VMEM),
        ],
        out_specs=(pl.BlockSpec(memory_space=pl.ANY), pl.BlockSpec(memory_space=pl.ANY)),
        scratch_shapes=[
            pltpu.VMEM((depth * width // block**2 + 1, block, block), jnp.bfloat16),
            pltpu.VMEM((2, capacity, block, block), jnp.bfloat16),
            pltpu.SemaphoreType.DMA((2, 4 if capacity % 32 == 0 else 1)),
        ],
        compiler_params=pltpu.CompilerParams(vmem_limit_bytes=56 << 20),
        cost_estimate=pl.CostEstimate(
            flops=4 * depth * width * turned.shape[1],
            bytes_accessed=4 * capacity * block * block,
            transcendentals=0,
        ),
    )(lists, counts, turned, delta)


def shards(tokens, gate_blocks, up_blocks, gate_list, gate_count, up_list, up_count, cotangent):
    owners = lax.axis_size("token")
    me = lax.axis_index("token")
    capacity, block = gate_blocks.shape[2:4]
    width = cotangent.shape[1]
    model = tokens.shape[1] * lax.axis_size("weight") * lax.axis_size("sub")
    depth = model // owners
    lists = jnp.stack([gate_list[me, 0], up_list[me, 0]])
    counts = jnp.stack([gate_count[me, 0], up_count[me, 0]])

    features = lax.all_gather(tokens, ("token", "weight"), axis=0)
    placed = place(lists, counts, gate_blocks[0, 0], up_blocks[0, 0], depth, width)
    hidden, turned, delta = exchange(features, placed, cotangent, owners)
    gate_grad, up_grad = block_grads(lists, counts, turned, delta, capacity, block)
    shape = (1, 1, capacity, block, block)
    return (hidden, gate_grad.reshape(shape), up_grad.reshape(shape))


def solution(mesh):
    return jax.shard_map(
        shards,
        mesh=mesh,
        in_specs=(
            P(("groups", "token"), ("weight", "sub")),
            P("token", ("weight", "sub"), None, None, None),
            P("token", ("weight", "sub"), None, None, None),
            P(None, ("weight", "sub"), None),
            P(None, ("weight", "sub")),
            P(None, ("weight", "sub"), None),
            P(None, ("weight", "sub")),
            P(("groups", "token"), ("weight", "sub")),
        ),
        out_specs=(
            P(("groups", "token"), ("weight", "sub")),
            P(("groups", "token"), ("weight", "sub"), None, None, None),
            P(("groups", "token"), ("weight", "sub"), None, None, None),
        ),
        check_vma=False,
    )
```
